32 devices in a mesh: gy: 2 (over y), gx: 4 (over z), hd: 4 (over x, core).
Axes of the slice: x: 2, y: 2, z: 4, core: 2. Of those that a mesh axis runs over, the one named last changes fastest.
Arguments:
- tokens: bfloat16 [32, 64, 1536], P('gy', 'gx'), may hold values from -6 to 6
- w_qkv: bfloat16 [1536, 3, 768], P(('gy', 'gx'), None, 'hd'), may hold values from -0.15625 to 0.15625
- rel_bias: float32 [12, 16, 16], P('hd'), may hold values from -6 to 300
- block_mask: int32 [4, 8], replicated, may hold values 0 or 1
- cotangent: bfloat16 [32, 64, 768], P('gy', 'gx', 'hd'), may hold values from -6 to 6
Outputs:
- attended: bfloat16 [32, 64, 768], P('gy', 'gx', 'hd')
- grad_tokens: bfloat16 [32, 64, 1536], P('gy', 'gx')
- grad_weight: float32 [1536, 3, 768], P(('gy', 'gx'), None, 'hd')
- grad_bias: float32 [12, 16, 16], P('hd')
The draws below stay inside these ranges and needn't reach their ends.
All inputs are finite; a program needn't handle non-finite values.
Results may differ from the reference program's by a relative error of at most 0.0087.
Values may be sent and summed in bfloat16 or wider, within the bound.
No kernel may reach another device: no remote copies, remote signals or barrier semaphores. Data moves between devices by JAX's collectives and lax.ppermute only.
A program may use at most 64 MiB of HBM per device.

```python
import math
import jax
import jax.numpy as jnp
from jax import lax

D = 1536
HEADS = 12
HDIM = 64
WIN = 16
MASK_BLOCK = 8
NH = 32
NW = 64


def draw_rel_bias(key, part):
    noise_key = jax.random.fold_in(key, 0)
    table_shape = (HEADS, WIN, WIN)
    return jnp.clip(jax.random.normal(noise_key, table_shape, jnp.float32), -6.0, 6.0)


def place_ends(values, key, low, high):
    place = [jax.random.randint(jax.random.fold_in(key, axis), (), 0, length) for axis, length in enumerate(values.shape)]
    widest = values.shape.index(max(values.shape))
    next_to = place[:widest] + [(place[widest] + 1) % values.shape[widest]] + place[widest + 1:]
    return values.at[tuple(place)].set(low).at[tuple(next_to)].set(high)


def levels(stream_key, extent, cuts, least, top_value):
    gain = 1.0
    for position, shards_of in cuts:
        draws = jax.random.uniform(jax.random.fold_in(jax.random.fold_in(stream_key, 6), position), (shards_of,), jnp.float32, least / len(cuts), top_value / len(cuts))
        gain = gain * jnp.repeat(jnp.exp(draws), extent[position] // shards_of).reshape((-1,) + (1,) * (len(extent) - 1 - position))
    return gain


def centred(stream_key, shape, deviation, bound, shards=(), kind=jnp.bfloat16):
    entries = deviation * jax.random.normal(stream_key, shape, jnp.float32)
    if shards:
        entries = entries * levels(stream_key, shape, shards, -0.22, 0.18)
    return jnp.clip(entries, -bound, bound).astype(kind)


def setup_inputs(seed: int = 0) -> dict:
    arg_keys = jax.random.split(jax.random.key(seed), 6)
    return {
        "tokens": centred(arg_keys[0], (NH, NW, D), 1.0, 6.0, ((0, 2), (1, 4))),
        "w_qkv": centred(arg_keys[1], (D, 3, HEADS * HDIM), D ** -0.5, 0.15625, ((0, 8), (2, 4))),
        "rel_bias": draw_rel_bias(jax.random.fold_in(arg_keys[5], 71), 0),
        "block_mask": place_ends((jax.random.randint(arg_keys[3], (NH // MASK_BLOCK, NW // MASK_BLOCK), 0, 4) < 3).astype(jnp.int32), jax.random.fold_in(arg_keys[3], 1), 0, 1),
        "cotangent": centred(arg_keys[4], (NH, NW, HEADS * HDIM), 1.0, 6.0, ((0, 2), (1, 4), (2, 4))),
    }


def head_pass(query, key, value, outer, bias, padded_valid):
    margin = WIN // 2
    score_scale = 1.0 / math.sqrt(HDIM)
    key_pad = jnp.pad(key, ((margin, margin), (margin, margin), (0, 0)))
    value_pad = jnp.pad(value, ((margin, margin), (margin, margin), (0, 0)))
    offsets = jnp.arange(WIN * WIN, dtype=jnp.int32)
    query_full = query.astype(jnp.float32)
    outer_full = outer.astype(jnp.float32)
    zero_index = jnp.int32(0)

    def score_at(offset):
        row_off = offset // WIN
        col_off = offset % WIN
        keys = lax.dynamic_slice(key_pad, (row_off, col_off, zero_index), (NH, NW, HDIM)).astype(jnp.float32)
        logits = lax.optimization_barrier(jnp.sum(query_full * keys, -1)) * score_scale + bias[row_off, col_off]
        seen = lax.dynamic_slice(padded_valid, (row_off, col_off), (NH, NW)) == 1
        centre = (row_off == margin) & (col_off == margin)
        return jnp.where(seen | centre, logits, -jnp.inf)
    logits = lax.map(score_at, offsets)
    top = lax.optimization_barrier(jnp.max(logits, 0))
    expo = jnp.exp(logits - top)
    weights = expo / lax.optimization_barrier(jnp.sum(expo, 0))
    weights_low = weights.astype(jnp.bfloat16)

    def forward_step(total, item):
        offset, weight_row = item
        row_off = offset // WIN
        col_off = offset % WIN
        values = lax.dynamic_slice(value_pad, (row_off, col_off, zero_index), (NH, NW, HDIM)).astype(jnp.float32)
        total = total + weight_row.astype(jnp.float32)[..., None] * values
        return (total, lax.optimization_barrier(jnp.sum(outer_full * values, -1)))
    attended, value_scores = lax.scan(forward_step, jnp.zeros((NH, NW, HDIM), jnp.float32), (offsets, weights_low))
    delta = lax.optimization_barrier(jnp.sum(weights * value_scores, 0))
    score_grad = weights * (value_scores - delta)
    bias_grad = lax.optimization_barrier(jnp.sum(score_grad, axis=(1, 2))).reshape(WIN, WIN)
    score_low = score_grad.astype(jnp.bfloat16)

    def backward_step(carry, item):
        query_grad, key_grad, value_grad = carry
        offset, score_row, weight_row = item
        row_off = offset // WIN
        col_off = offset % WIN
        start = (row_off, col_off, zero_index)
        keys = lax.dynamic_slice(key_pad, start, (NH, NW, HDIM)).astype(jnp.float32)
        score_full = score_row.astype(jnp.float32)[..., None]
        query_grad = query_grad + score_full * keys
        key_piece = lax.dynamic_slice(key_grad, start, (NH, NW, HDIM)) + score_full * query_full
        key_grad = lax.dynamic_update_slice(key_grad, key_piece, start)
        value_piece = lax.dynamic_slice(value_grad, start, (NH, NW, HDIM)) + weight_row.astype(jnp.float32)[..., None] * outer_full
        value_grad = lax.dynamic_update_slice(value_grad, value_piece, start)
        return ((query_grad, key_grad, value_grad), None)
    padded_zeros = jnp.zeros((NH + 2 * margin, NW + 2 * margin, HDIM), jnp.float32)
    init = (jnp.zeros((NH, NW, HDIM), jnp.float32), padded_zeros, padded_zeros)
    (query_grad, key_grad, value_grad), unused = lax.scan(backward_step, init, (offsets, score_low, weights_low))
    query_grad = query_grad * score_scale
    key_grad = key_grad[margin:margin + NH, margin:margin + NW] * score_scale
    value_grad = value_grad[margin:margin + NH, margin:margin + NW]
    return (attended, query_grad, key_grad, value_grad, bias_grad)

def merge_heads(stacked):
    return jnp.moveaxis(stacked, 0, 2).reshape(NH, NW, HEADS * HDIM)

def reference(tokens, w_qkv, rel_bias, block_mask, cotangent):
    columns = HEADS * HDIM
    flat = tokens.reshape(NH * NW, D)
    weight_flat = w_qkv.reshape(D, 3 * columns)
    projected = jnp.dot(flat, weight_flat, preferred_element_type=jnp.float32).astype(jnp.bfloat16)
    parts = jnp.moveaxis(projected.reshape(NH, NW, 3, HEADS, HDIM), (2, 3), (0, 1))
    outer = jnp.moveaxis(cotangent.reshape(NH, NW, HEADS, HDIM), 2, 0)
    valid = jnp.repeat(jnp.repeat(block_mask, MASK_BLOCK, axis=0), MASK_BLOCK, axis=1)
    padded_valid = jnp.pad(valid, WIN // 2)

    def run_head(item):
        return head_pass(item[0], item[1], item[2], item[3], item[4], padded_valid)
    attended, query_grad, key_grad, value_grad, bias_grad = lax.map(run_head, (parts[0], parts[1], parts[2], outer, rel_bias))
    attended_out = merge_heads(attended).astype(jnp.bfloat16)
    grads = jnp.stack([merge_heads(query_grad), merge_heads(key_grad), merge_heads(value_grad)], axis=2).astype(jnp.bfloat16)
    grads_flat = grads.reshape(NH * NW, 3 * columns)
    grad_tokens = jnp.dot(grads_flat, weight_flat.T, preferred_element_type=jnp.float32).astype(jnp.bfloat16).reshape(NH, NW, D)
    grad_weight = jnp.dot(flat.T, grads_flat, preferred_element_type=jnp.float32).reshape(D, 3, columns)
    return (attended_out, grad_tokens, grad_weight, bias_grad)
```

```python
import functools
import math

import jax
import jax.numpy as jnp
from jax import lax
from jax.experimental import pallas as pl
from jax.experimental.pallas import tpu as pltpu
from jax.sharding import PartitionSpec as P

MASK_BLOCK = 8
F32 = jnp.float32
BF16 = jnp.bfloat16
VMEM = pl.BlockSpec(memory_space=pltpu.VMEM)
SMEM = pl.BlockSpec(memory_space=pltpu.SMEM)


def xor_pairs(count, step):
    return [(i, i ^ step) for i in range(count) if i ^ step < count]


def side_pairs(count, first):
    low = range(first, count - 1, 2)
    return [(i, i + 1) for i in low] + [(i + 1, i) for i in low]


def swap(value, axis, step):
    return lax.ppermute(value, axis, xor_pairs(lax.axis_size(axis), step))


def side_swaps(axis, to_low, to_high):
    count = lax.axis_size(axis)
    odd = lax.axis_index(axis) % 2 == 1
    first = lax.ppermute(jnp.where(odd, to_low, to_high), axis, side_pairs(count, 0))
    if count == 2:
        return first, None
    second = lax.ppermute(jnp.where(odd, to_high, to_low), axis, side_pairs(count, 1))
    return first, second


def by_side(axis, first, second):
    odd = lax.axis_index(axis) % 2 == 1
    if second is None:
        second = jnp.zeros_like(first)
    return jnp.where(odd, first, second), jnp.where(odd, second, first)


def call(kernel, outs, *args, scratch=(), smem=0, name=None, flops=0, vmem=40 << 20, aliases=None):
    moved = sum(math.prod(a.shape) * a.dtype.itemsize for a in args)
    moved += sum(math.prod(o.shape) * o.dtype.itemsize for o in outs)
    return pl.pallas_call(
        kernel,
        out_shape=outs,
        in_specs=[SMEM] * smem + [VMEM] * (len(args) - smem),
        out_specs=[VMEM] * len(outs),
        scratch_shapes=list(scratch),
        name=name,
        input_output_aliases=aliases or {},
        cost_estimate=pl.CostEstimate(flops=flops, bytes_accessed=moved, transcendentals=0),
        compiler_params=pltpu.CompilerParams(vmem_limit_bytes=vmem),
    )(*args)


def shape(dims, dtype):
    return jax.ShapeDtypeStruct(tuple(dims), dtype)


def pack_rows(planes, out_ref, cast):
    rows, cols = planes[0].shape
    rest = cols - 128
    for c in range(3):
        out_ref[c * rows : (c + 1) * rows] = planes[c][:, :128].astype(cast)
    tails = [planes[c][:, 128:] for c in range(3)]
    out_ref[3 * rows : 4 * rows] = jnp.concatenate([tails[0], tails[1]], -1).astype(cast)
    half = rows // 2
    out_ref[4 * rows :] = jnp.concatenate([tails[2][:half], tails[2][half:]], -1).astype(cast)


def unpack_rows(packed, rows):
    half = rows // 2
    pair = packed[3 * rows : 4 * rows]
    last = packed[4 * rows :]
    tails = [pair[:, :64], pair[:, 64:], jnp.concatenate([last[:, :64], last[:, 64:]], 0)]
    return [
        jnp.concatenate([packed[c * rows : (c + 1) * rows], tails[c]], -1) for c in range(3)
    ]


def pack_kernel(w_ref, out_ref):
    pack_rows([w_ref[c].astype(F32) for c in range(3)], out_ref, BF16)


def unpack_kernel(rows, in_ref, out_ref):
    planes = unpack_rows(in_ref[...], rows)
    for c in range(3):
        out_ref[c] = planes[c]


def assemble_kernel(rows, place_ref, *refs):
    pieces, outs = refs[:-3], refs[-3:]
    for piece, ref in enumerate(pieces):
        start = pl.multiple_of(place_ref[piece] * rows, rows)
        planes = unpack_rows(ref[...].astype(F32), rows)
        for c in range(3):
            outs[c][pl.ds(start, rows)] = planes[c].astype(BF16)


def bias_kernel(heads, window, q_rows, q_cols, key_rows, key_cols, rel_ref, valid_ref, out_ref, part):
    margin = window // 2
    block_count = out_ref.shape[1]
    tile = (key_cols, q_rows * q_cols)
    lane = lax.broadcasted_iota(jnp.int32, tile, 1)
    col_off = lax.broadcasted_iota(jnp.int32, tile, 0) - lane % q_cols
    q_row = lane // q_cols
    minus = jnp.full(tile, -jnp.inf, F32)
    hits = [col_off == b for b in range(window)]
    for h in range(heads):

        def row(a, unused, h=h):
            total = minus
            for b in range(window):
                total = jnp.where(hits[b], rel_ref[h, a * window + b], total)
            part[a] = total
            return unused

        lax.fori_loop(0, window, row, 0)
        for key_row in range(key_rows):
            total = minus
            for i in range(q_rows):
                a = key_row - i
                if 0 <= a < window:
                    total = jnp.where(q_row == i, part[a], total)
            own = (q_row == key_row - margin) & (col_off == margin)
            for block in range(block_count):
                low = (block * q_rows + key_row) * key_cols
                seen = valid_ref[low : low + key_cols] > 0.5
                out_ref[h, block, key_row * key_cols : (key_row + 1) * key_cols] = jnp.where(
                    seen | own, total, -jnp.inf
                )


def bias_grad_kernel(heads, window, q_rows, q_cols, key_rows, key_cols, st_ref, out_ref):
    tile = (key_cols, q_rows * q_cols)
    lane = lax.broadcasted_iota(jnp.int32, tile, 1)
    col_off = lax.broadcasted_iota(jnp.int32, tile, 0) - lane % q_cols
    q_row = lane // q_cols
    hits = [col_off == b for b in range(window)]
    for h in range(heads):

        def row(a, unused, h=h):
            total = jnp.zeros(tile, F32)
            for i in range(q_rows):
                start = pl.multiple_of((a + i) * key_cols, key_cols)
                total = jnp.where(q_row == i, st_ref[h, pl.ds(start, key_cols)], total)
            sums = [jnp.sum(jnp.where(hits[b], total, 0.0), 0, keepdims=True) for b in range(window)]
            start = pl.multiple_of(a * window, window)
            out_ref[h, pl.ds(start, window)] = jnp.concatenate(sums, 0)
            return unused

        lax.fori_loop(0, window, row, 0)


def dot(a, b, dims):
    return lax.dot_general(a, b, (dims, ((), ())), preferred_element_type=F32)


def attention_kernel(
    heads, head_dim, block, keys, step, tok_ref, own_ref, wq_ref, wk_ref, wv_ref, cot_ref, bias_ref,
    att_ref, dq_ref, dk_ref, dv_ref, st_ref, q_s, k_s, v_s, kt_s, vt_s, at_s, dqt_s,
):
    scale = 1.0 / math.sqrt(head_dim)
    plain = ((1,), (0,))
    last = ((1,), (1,))
    tokens = tok_ref[...]
    k = dot(tokens, wk_ref[...], plain)
    k_s[...] = k.astype(BF16)
    kt_s[...] = k.T.astype(BF16)
    v = dot(tokens, wv_ref[...], plain)
    v_s[...] = v.astype(BF16)
    vt_s[...] = v.T.astype(BF16)
    q = dot(own_ref[...], wq_ref[...], plain).astype(BF16)
    q_s[...] = (q.astype(F32) * scale).astype(BF16)
    dk_ref[...] = jnp.zeros_like(dk_ref)
    dv_ref[...] = jnp.zeros_like(dv_ref)
    blocks = q_s.shape[0] // block
    lane = lax.broadcasted_iota(jnp.int32, (block, q_s.shape[1]), 1)
    for h in range(heads):
        here = (lane >= h * head_dim) & (lane < (h + 1) * head_dim)
        head = slice(h * head_dim, (h + 1) * head_dim)
        for b in range(blocks):
            queries = slice(b * block, (b + 1) * block)
            span = slice(b * step, b * step + keys)
            q_h = jnp.where(here, q_s[queries], 0)
            out_h = jnp.where(here, cot_ref[queries], 0)
            logits = dot(k_s[span], q_h, last) + bias_ref[h, b]
            top = jnp.max(logits, 0, keepdims=True)
            expo = jnp.exp(logits - top)
            weights = expo * (1.0 / jnp.sum(expo, 0, keepdims=True))
            weights_low = weights.astype(BF16)
            value_scores = dot(v_s[span], out_h, last)
            delta = jnp.sum(weights * value_scores, 0, keepdims=True)
            score = weights * (value_scores - delta)
            if b == 0:
                st_ref[h] = score
            else:
                st_ref[h] += score
            score_low = score.astype(BF16)
            at_s[head, queries] = dot(vt_s[head, span], weights_low, plain)
            dqt_s[head, queries] = dot(kt_s[head, span], score_low, plain)
            dk_ref[span] += dot(score_low, q_h, plain)
            dv_ref[span] += dot(weights_low, out_h, plain)
    att_ref[...] = at_s[...].T.astype(BF16)
    dq_ref[...] = (dqt_s[...].T * scale).astype(BF16)


def weight_grad_kernel(rows, packed, tok_ref, own_ref, dq_ref, dk_ref, dv_ref, place_ref, out_ref, *scratch):
    first = ((0,), (0,))
    parts = scratch if packed else [out_ref.at[c] for c in range(3)]
    parts[0][...] = dot(own_ref[...], dq_ref[...], first)
    parts[1][...] = dot(tok_ref[...], dk_ref[...].astype(BF16), first)
    parts[2][...] = dot(tok_ref[...], dv_ref[...].astype(BF16), first)
    if packed:
        for piece in range(out_ref.shape[0]):
            start = pl.multiple_of(place_ref[piece] * rows, rows)
            planes = [parts[c][pl.ds(start, rows)] for c in range(3)]
            pack_rows(planes, out_ref.at[piece], F32)


def token_grad_kernel(dq_ref, dkv_ref, wq_ref, wk_ref, wv_ref, out_ref):
    last = ((1,), (1,))
    cols = dq_ref.shape[1]
    total = dot(dq_ref[...], wq_ref[...], last)
    total += dot(dkv_ref[0], wk_ref[...], last)
    out_ref[...] = total + dot(dkv_ref[1], wv_ref[...], last)


def exchange_weights(own):
    half = own.shape[0] // 2
    z2 = swap(own, "gx", 2)
    z1 = swap(own, "gx", 1)
    y0 = swap(own, "gy", 1)
    by_z = swap(jnp.concatenate([z2, y0[:half]]), "gx", 1)
    by_y = swap(jnp.concatenate([z2, z1[half:]]), "gy", 1)
    z3, y1_top = by_z[: 2 * half], by_z[2 * half :]
    y2, y1_low = by_y[: 2 * half], by_y[2 * half :]
    y3_top = swap(y2[:half], "gx", 1)
    y3_low = swap(z3[half:], "gy", 1)
    y1 = jnp.concatenate([y1_top, y1_low])
    y3 = jnp.concatenate([y3_top, y3_low])
    return [own, z1, z2, z3, y0, y1, y2, y3]


def scatter_weights(acc):
    half = acc.shape[1] // 2
    low = lambda x: x.astype(BF16)
    up = lambda x: x.astype(F32)
    own, z1, z2, z3, y0, y1, y2, y3 = [acc[i] for i in range(8)]
    a_top = up(swap(low(y3[:half]), "gx", 1))
    a_low = up(swap(low(y3[half:]), "gy", 1))
    by_z = jnp.concatenate([low(z3[:half]), low(z3[half:] + a_low), low(y1[:half])])
    by_y = jnp.concatenate([low(y2[:half] + a_top), low(y2[half:]), low(y1[half:])])
    by_z = up(swap(by_z, "gx", 1))
    by_y = up(swap(by_y, "gy", 1))
    z2 = z2 + by_z[: 2 * half] + by_y[: 2 * half]
    z1 = jnp.concatenate([z1[:half], z1[half:] + by_y[2 * half :]])
    y0 = jnp.concatenate([y0[:half] + by_z[2 * half :], y0[half:]])
    total = own + up(swap(low(z2), "gx", 2))
    total = total + up(swap(low(z1), "gx", 1))
    return total + up(swap(low(y0), "gy", 1))


def sum_tiles(value, swaps):
    if not swaps:
        return lax.psum(value, ("gy", "gx"))
    for axis, step in (("gy", 1), ("gx", 1), ("gx", 2)):
        value = value + swap(value, axis, step)
    return value


def sum_heads(partial):
    count = lax.axis_size("hd")
    if count != 4:
        return lax.psum(partial, "hd").astype(BF16)
    rows = partial.shape[0] // 2
    even = lax.axis_index("hd") % 2 == 0
    send = jnp.where(even, partial[rows:], partial[:rows]).astype(BF16)
    keep = jnp.where(even, partial[:rows], partial[rows:])
    part = keep + swap(send, "hd", 1).astype(F32)
    part = (part + swap(part.astype(BF16), "hd", 2).astype(F32)).astype(BF16)
    other = swap(part, "hd", 1)
    return jnp.where(even, jnp.concatenate([part, other]), jnp.concatenate([other, part]))


def extend_tokens(tokens, margin):
    rows, cols, width = tokens.shape
    count = lax.axis_size("gy")
    pair = lax.axis_size("hd") % 2 == 0
    odd = lax.axis_index("hd") % 2 == 1
    part = width
    sent = tokens
    if pair:
        part = width // 2
        sent = jnp.where(odd, tokens[:, :, part:], tokens[:, :, :part])

    def both(value):
        if not pair or value is None:
            return value
        other = swap(value, "hd", 1)
        return jnp.where(
            odd, jnp.concatenate([other, value], -1), jnp.concatenate([value, other], -1)
        )

    first, second = side_swaps("gy", sent[:margin], sent[rows - margin :])
    low, high = by_side("gy", first, second)
    tall = jnp.concatenate([low, sent, high], 0)
    start = 0
    if count == 2:
        start = margin * (1 - lax.axis_index("gy"))
        tall = lax.dynamic_slice(tall, (start, 0, 0), (rows + margin, cols, part))
    left, right = side_swaps("gx", tall[:, :margin], tall[:, cols - margin :])
    low, high = by_side("gy", both(first), both(second))
    middle = jnp.concatenate([low, tokens, high], 0)
    left, right = by_side("gx", both(left), both(right))
    if count == 2:
        whole = jnp.zeros((rows + 2 * margin, margin, width), tokens.dtype)
        left = lax.dynamic_update_slice(whole, left, (start, 0, 0))
        right = lax.dynamic_update_slice(whole, right, (start, 0, 0))
    return jnp.concatenate([left, middle, right], 1)


def fold_halo(ext, rows, cols, margin):
    def fold(value, axis, dim, size):
        odd = lax.axis_index(axis) % 2 == 1
        cut = lambda a, b: lax.slice_in_dim(value, a, b, axis=dim)
        own = cut(margin, margin + size)
        to_low, to_high = cut(0, margin), cut(margin + size, 2 * margin + size)
        first, second = side_swaps(axis, to_low.astype(BF16), to_high.astype(BF16))
        low, high = by_side(axis, first, second)
        return own + jnp.concatenate([low, high], dim).astype(F32)

    tall = fold(ext, "gy", 1, rows)
    return fold(tall, "gx", 2, cols)


def on_device(tokens, w_qkv, rel_bias, block_mask, cotangent):
    tile_rows, tile_cols, width = tokens.shape
    heads_here, window = (rel_bias.shape[0], rel_bias.shape[1])
    margin = window // 2
    group_cols = cotangent.shape[2]
    head_dim = group_cols // heads_here
    queries = tile_rows * tile_cols
    ext_rows = tile_rows + 2 * margin
    ext_cols = tile_cols + 2 * margin
    weight_rows = w_qkv.shape[0]
    gy_count, gx_count = lax.axis_size("gy"), lax.axis_size("gx")
    swaps = (gy_count, gx_count) == (2, 4) and group_cols == 192
    gy, gx = lax.axis_index("gy"), lax.axis_index("gx")

    planes = jnp.transpose(w_qkv, (1, 0, 2))
    packed_rows = weight_rows * 3 * group_cols // 128
    if swaps:
        packed = call(pack_kernel, [shape((packed_rows, 128), BF16)], planes, name="pack")[0]
        places = jnp.stack([(gy ^ (i // 4)) * 4 + (gx ^ (i % 4)) for i in range(8)]).astype(jnp.int32)
        pieces = exchange_weights(packed)
        weights = call(
            functools.partial(assemble_kernel, weight_rows),
            [shape((width, group_cols), BF16)] * 3,
            places, *pieces, smem=1, name="assemble",
        )
    else:
        places = jnp.zeros((8,), jnp.int32)
        whole = lax.all_gather(w_qkv, ("gy", "gx"), axis=0, tiled=True)
        weights = [whole[:, c] for c in range(3)]

    extended = extend_tokens(tokens, margin).reshape(ext_rows * ext_cols, width)
    flat = tokens.reshape(queries, width)
    outer = cotangent.reshape(queries, group_cols)

    q_rows = 128 // tile_cols
    block = q_rows * tile_cols
    blocks = tile_rows // q_rows
    key_rows = q_rows + 2 * margin
    keys = key_rows * ext_cols
    valid = jnp.repeat(jnp.repeat(block_mask, MASK_BLOCK, axis=0), MASK_BLOCK, axis=1)
    ext_valid = lax.dynamic_slice(
        jnp.pad(valid, margin), (gy * tile_rows, gx * tile_cols), (ext_rows, ext_cols)
    )
    ext_valid = jnp.broadcast_to(
        (ext_valid == 1).astype(F32).reshape(ext_rows * ext_cols, 1), (ext_rows * ext_cols, block)
    )
    sizes = (heads_here, window, q_rows, tile_cols, key_rows, ext_cols)
    bias_map = call(
        functools.partial(bias_kernel, *sizes),
        [shape((heads_here, blocks, keys, block), F32)],
        rel_bias.reshape(heads_here, window * window), ext_valid, smem=1, name="bias_map",
        scratch=[pltpu.VMEM((window, ext_cols, block), F32)],
    )[0]

    ext = ext_rows * ext_cols
    attended, dq, dk, dv, score_total = call(
        functools.partial(attention_kernel, heads_here, head_dim, block, keys, q_rows * ext_cols),
        [
            shape((queries, group_cols), BF16),
            shape((queries, group_cols), BF16),
            shape((ext, group_cols), F32),
            shape((ext, group_cols), F32),
            shape((heads_here, keys, block), F32),
        ],
        extended, flat, *weights, outer, bias_map, name="attention", flops=6 << 30,
        scratch=[
            pltpu.VMEM((queries, group_cols), BF16),
            pltpu.VMEM((ext, group_cols), BF16),
            pltpu.VMEM((ext, group_cols), BF16),
            pltpu.VMEM((group_cols, ext), BF16),
            pltpu.VMEM((group_cols, ext), BF16),
            pltpu.VMEM((group_cols, queries), F32),
            pltpu.VMEM((group_cols, queries), F32),
        ],
    )

    grads = jnp.stack([dk, dv]).reshape(2, ext_rows, ext_cols, group_cols)
    own_grads = fold_halo(grads, tile_rows, tile_cols, margin).astype(BF16)
    token_partial = call(
        token_grad_kernel, [shape((queries, width), F32)],
        dq, own_grads.reshape(2, queries, group_cols), *weights, name="token_grad", flops=1 << 30,
    )[0]
    grad_tokens = sum_heads(token_partial).reshape(tile_rows, tile_cols, width)

    if swaps:
        product = pl.pallas_call(
            functools.partial(weight_grad_kernel, weight_rows, True),
            out_shape=[shape((8, packed_rows, 128), F32)],
            in_specs=[VMEM] * 5 + [SMEM],
            out_specs=[VMEM],
            scratch_shapes=[pltpu.VMEM((width, group_cols), F32)] * 3,
            name="weight_grad",
            cost_estimate=pl.CostEstimate(flops=2 << 30, bytes_accessed=12 << 20, transcendentals=0),
            compiler_params=pltpu.CompilerParams(vmem_limit_bytes=40 << 20),
        )(extended, flat, dq, dk, dv, places)[0]
        total = scatter_weights(product)
        grad_weight = call(
            functools.partial(unpack_kernel, weight_rows),
            [shape((3, weight_rows, group_cols), F32)], total, name="unpack",
        )[0]
    else:
        product = pl.pallas_call(
            functools.partial(weight_grad_kernel, weight_rows, False),
            out_shape=[shape((3, width, group_cols), F32)],
            in_specs=[VMEM] * 5 + [SMEM],
            out_specs=[VMEM],
            name="weight_grad",
            compiler_params=pltpu.CompilerParams(vmem_limit_bytes=40 << 20),
        )(extended, flat, dq, dk, dv, places)[0]
        grad_weight = lax.psum_scatter(product, ("gy", "gx"), scatter_dimension=1, tiled=True)
    grad_weight = jnp.transpose(grad_weight, (1, 0, 2))

    bias_sums = call(
        functools.partial(bias_grad_kernel, *sizes),
        [shape((heads_here, window * window, block), F32)], score_total, name="bias_grad",
    )[0]
    grad_bias = sum_tiles(jnp.sum(bias_sums, -1).reshape(heads_here, window, window), swaps)
    attended = attended.reshape(tile_rows, tile_cols, group_cols)
    return (attended, grad_tokens, grad_weight, grad_bias)


def solution(mesh):
    return jax.shard_map(
        on_device,
        mesh=mesh,
        in_specs=(
            P("gy", "gx", None),
            P(("gy", "gx"), None, "hd"),
            P("hd", None, None),
            P(),
            P("gy", "gx", "hd"),
        ),
        out_specs=(
            P("gy", "gx", "hd"),
            P("gy", "gx", None),
            P(("gy", "gx"), None, "hd"),
            P("hd", None, None),
        ),
        check_vma=False,
    )
```
